32 devices in a mesh: groups: 2 (over x), dp: 8 (over z, y), split: 2 (over core).
Axes of the slice: x: 2, y: 2, z: 4, core: 2. Of those that a mesh axis runs over, the one named last changes fastest.
Arguments:
- embeddings: bfloat16 [65536, 512], P(('groups', 'dp', 'split')), parts along dimension 0, may hold values from -6 to 6
- assignment: int32 [65536, 1], P(('groups', 'dp', 'split')), parts along dimension 0, may hold values from 0 to 15; in each aligned block of 2048 rows (0 to 2047, 2048 to 4095, ...) at most 192 rows name the same one
- order_key: int32 [65536], P(('groups', 'dp', 'split')), parts along dimension 0, may hold values from 0 to 32767, each once
Outputs:
- nearest: float32 [65536], P(('groups', 'dp', 'split')), parts along dimension 0
The draws below stay inside these ranges and needn't reach their ends.
There are 2 independent parts, one for each index of `groups`. The reference program is written for one: setup_inputs(seed, part) draws one part's arguments, and reference() takes and returns one part's arrays. A program takes and returns all parts, laid end to end along the dimension named above; each array names one. Nothing has to cross between parts.
Inputs may be any that keep to these rules, and one draw needn't show every extreme that they name: `assignment`: in each device's 2048 rows no cluster has more than 192 rows, and some cluster has exactly 192. `order_key`: all values within a part are distinct.
All inputs are finite; a program needn't handle non-finite values.
Results may differ from the reference program's by a relative error of at most 0.0013.
Values may be sent and summed in bfloat16 or wider, within the bound.
A program may use at most 64 MiB of HBM per device.

```python
import math
import jax
import jax.numpy as jnp
import numpy as np
from jax import lax

D = 512
ROWS_DEV = 2048
CLUSTERS = 16
MOST = 192
ROWS = 32768
N_DP = 8
N_SPLIT = 2


def levels(key, extent, pieces, least, top_value):
    def one(dim, blocks):
        steps = jax.random.uniform(jax.random.fold_in(jax.random.fold_in(key, 6), dim), (blocks,), jnp.float32, least / len(pieces), top_value / len(pieces))
        return jnp.repeat(jnp.exp(steps), extent[dim] // blocks).reshape((-1,) + (1,) * (len(extent) - dim - 1))

    loudness = one(*pieces[0])
    for cut in pieces[1:]:
        loudness = loudness * one(*cut)
    return loudness


def routed_block(key, own, number, rows, count, top, reach, lean):
    order = jax.random.permutation(key, count)
    crowded, usual = load_shares(count, rows * top, reach, lean, True), load_shares(count, rows * top, reach, lean, False)
    places = jnp.arange(count)

    def named(tallies, rotation):
        used = int((tallies > 0).sum())
        fixed = max(1, used // 4)
        shifted = fixed + (places - fixed + rotation * (used - fixed)) % max(1, count - fixed)
        return jnp.zeros((count,), jnp.int32).at[order[jnp.where(places < fixed, places, shifted)]].set(jnp.asarray(tallies, jnp.int32))

    tallies = jnp.where(number % 4 == 0, named(crowded, number // 4), named(usual, number - number // 4 - 1))
    mixed = jax.random.permutation(jax.random.fold_in(own, 3), count)
    donor, receiver = mixed[0:count // 2 * 2:2], mixed[1:count // 2 * 2:2]
    slack = jnp.minimum(tallies[donor] - 1, reach - tallies[receiver]) // 2
    slack = jnp.where((donor == order[0]) | (receiver == order[0]) | (tallies[receiver] == 0), 0, jnp.maximum(slack, 0))
    shifted = jax.random.randint(jax.random.fold_in(own, 4), (count // 2,), 0, 1 << 20) % (slack + 1)
    tallies = tallies.at[donor].add(-shifted).at[receiver].add(shifted)
    labels = jnp.searchsorted(jnp.cumsum(tallies), jnp.arange(rows * top), side="right").astype(jnp.int32)
    table = labels.reshape(top, rows).T
    table = table[jax.random.permutation(jax.random.fold_in(own, 1), rows)]
    rotation = jax.random.randint(jax.random.fold_in(own, 2), (rows, 1), 0, top)
    return jnp.take_along_axis(table, (jnp.arange(top)[None, :] + rotation) % top, axis=1)


def load_shares(amount, total, limit, lean, full):
    portions = [(1 << 20) // math.isqrt(standing ** lean) + 1 for standing in range(1, amount + 1)]
    largest = limit if full else min(limit, max(-(-total // amount), total * portions[0] // sum(portions)))
    least = 1 if total - largest >= amount - 1 else 0
    given, spare = [largest] + [least] * (amount - 1), total - largest - least * (amount - 1)
    while spare > 0:
        free = [i for i in range(1, amount) if given[i] < largest] or [i for i in range(1, amount) if given[i] < limit]
        mass, remaining = sum([portions[i] for i in free]), spare
        for i in free:
            addition = min(limit - given[i], max(1, remaining * portions[i] // mass), spare)
            given[i] = given[i] + addition
            spare = spare - addition
    return np.array(given)


def noise(key, shape, scale, bound, pieces=(), kind=jnp.bfloat16):
    level = levels(key, shape, pieces, -0.22, 0.18) if pieces else 1.0
    entries = jax.random.normal(key, shape, jnp.float32) * scale * level
    return jnp.minimum(jnp.maximum(entries, -bound), bound).astype(kind)


def setup_inputs(seed: int = 0, part: int = 0) -> dict:
    streams_of = jax.random.split(jax.random.key(seed), 4)
    own_keys = jax.random.split(jax.random.fold_in(streams_of[3], part), 4)
    embeddings = noise(own_keys[0], (ROWS, D), 1.0, 6.0, ((0, 16),))
    assignment_keys = jax.random.split(jax.random.fold_in(own_keys[1], 1), ROWS // ROWS_DEV)
    assignment_turns = jax.random.permutation(jax.random.fold_in(own_keys[1], 3), ROWS // ROWS_DEV)
    assignment = jax.vmap(lambda own, number: routed_block(jax.random.fold_in(own_keys[1], 2), own, number, ROWS_DEV, CLUSTERS, 1, MOST, 2))(assignment_keys, assignment_turns).reshape((ROWS, 1))
    order_key = jax.random.permutation(own_keys[2], ROWS).astype(jnp.int32)
    return {"embeddings": embeddings, "assignment": assignment, "order_key": order_key}


def reference(embeddings, assignment, order_key):
    values = embeddings.astype(jnp.float32)
    scale = lax.rsqrt(lax.optimization_barrier(jnp.sum(values * values, axis=1, keepdims=True)) + 1e-06)
    unit = (values * scale).astype(jnp.bfloat16).astype(jnp.float32)
    cluster = assignment[:, 0].astype(jnp.int32)
    capacity = N_SPLIT * N_DP * MOST
    ordering = jnp.argsort(cluster, stable=True).astype(jnp.int32)
    sorted_cluster = cluster[ordering]
    onehot = (cluster[:, None] == jnp.arange(CLUSTERS, dtype=jnp.int32)[None, :]).astype(jnp.int32)
    counts = lax.optimization_barrier(jnp.sum(onehot, axis=0))
    starts = (jnp.cumsum(counts) - counts).astype(jnp.int32)
    padded_unit = jnp.concatenate([unit[ordering], jnp.zeros((capacity, D), unit.dtype)], axis=0)
    padded_key = jnp.concatenate([order_key[ordering].astype(jnp.int32), jnp.zeros((capacity,), jnp.int32)], axis=0)
    padded_cluster = jnp.concatenate([sorted_cluster, jnp.full((capacity,), -1, jnp.int32)], axis=0)

    def one_cluster(index):
        begin = starts[index]
        block = lax.dynamic_slice(padded_unit, (begin, jnp.int32(0)), (capacity, D))
        keys = lax.dynamic_slice(padded_key, (begin,), (capacity,))
        members = lax.dynamic_slice(padded_cluster, (begin,), (capacity,))
        sims = jnp.dot(block, block.T, precision=lax.Precision.HIGHEST)
        allowed = (members[None, :] == index) & (keys[None, :] < keys[:, None])
        return lax.optimization_barrier(jnp.max(jnp.where(allowed, sims, -1.0), axis=1))
    table = lax.map(one_cluster, jnp.arange(CLUSTERS, dtype=jnp.int32))
    position = jnp.arange(ROWS, dtype=jnp.int32) - starts[sorted_cluster]
    result_sorted = table[sorted_cluster, position]
    nearest = jnp.zeros((ROWS,), result_sorted.dtype).at[ordering].set(result_sorted)
    return nearest
```

```python
import functools

import jax
import jax.numpy as jnp
from jax import lax
from jax.experimental import pallas as pl
from jax.experimental.pallas import tpu as pltpu
from jax.sharding import PartitionSpec as P

epsilon = 1e-06
MESH = pl.DeviceIdType.MESH
NT = (((1,), (1,)), ((), ()))
BLOCK = 256
SUB = 8
GROUP = 5


def xor(a, b, n):
    total, bit = 0, 1
    while bit < n:
        p, q = (a // bit) % 2, (b // bit) % 2
        total = total + (p + q - 2 * p * q) * bit
        bit *= 2
    return total


def flip(a, b, n):
    total, bit = 0, 1
    while bit < n:
        p = (a // bit) % 2
        total = total + (1 - p if b & bit else p) * bit
        bit *= 2
    return total


def entry(values, i):
    n, total = len(values), values[0] + i
    for k in range(1, n):
        jump = values[k] - values[k - 1] - 1
        if jump:
            total = total + jump * lax.div(i + (n - k), n)
    return total


def orders(n):
    q = n // 4
    same, near, far2, far3 = (list(range(max(1, i * q), i * q + q)) for i in range(4))
    send_outer = far2 + same + near + far3
    send_inner = far3[:2] + far2 + same + near + far3[2:]
    take_outer = [0] + same + near + far2 + far3
    take_inner = [0] + same + far3[:2] + far2 + near + far3[2:]
    return send_outer + [0], send_inner + [0], take_outer, take_inner


def kernel(n, n_split, most, rows_hbm, cluster_hbm, key_hbm, out_ref,
           rows_ref, cluster_ref, key_ref, fetch_sem, slot_ref, send, send_key, recv, recv_key, lane_key, sub_key, best, gather, back_send, back, by_rank,
           row_ssem, row_rsem, key_ssem, key_rsem, back_ssem, back_rsem, go):
    f32, bf16, i32 = jnp.float32, jnp.bfloat16, jnp.int32
    rows = rows_ref.shape[0]
    quarter = n // 4
    me = lax.axis_index("dp") * n_split + lax.axis_index("split")
    inner = (me // quarter // 2 + me // quarter) % 2
    barrier = pltpu.get_barrier_semaphore()

    def place_of(partner):
        return {"dp": partner // n_split, "split": partner % n_split}

    def device(offset):
        return place_of(flip(me, offset, n) if isinstance(offset, int) else xor(me, offset, n))

    def greet(offset):
        pl.semaphore_signal(barrier, inc=1, device_id=device(offset), device_id_type=MESH)

    @pl.when(inner == 1)
    def _():
        for offset in [3 * quarter, 3 * quarter + 1] + list(range(3 * quarter - 1, quarter - 1, -1)):
            greet(offset)

    @pl.when(inner == 0)
    def _():
        for offset in list(range(n - 1, 3 * quarter - 1, -1)) + list(range(1, quarter)):
            greet(offset)

    fetches = [
        pltpu.make_async_copy(cluster_hbm, cluster_ref, fetch_sem.at[0]),
        pltpu.make_async_copy(key_hbm, key_ref, fetch_sem.at[1]),
        pltpu.make_async_copy(rows_hbm, rows_ref, fetch_sem.at[2]),
    ]
    for fetch in fetches:
        fetch.start()

    send_outer, send_inner, take_outer, take_inner = orders(n)

    def either(outer_values, inner_values, i):
        first, second = entry(outer_values, i), entry(inner_values, i)
        return first + (second - first) * inner

    def sent(i):
        return either(send_outer, send_inner, i)

    def taken(i):
        return either(take_outer, take_inner, i)

    fetches[0].wait()
    before = (lax.broadcasted_iota(i32, (BLOCK, BLOCK), 0) < lax.broadcasted_iota(i32, (BLOCK, BLOCK), 1))
    before = jnp.where(before, 1.0, 0.0).astype(bf16)
    carry = jnp.zeros((n, 1), f32)
    for start in range(0, rows, BLOCK):
        here = cluster_ref[:, start:start + BLOCK]
        onehot = jnp.where(lax.broadcasted_iota(i32, (n, BLOCK), 0) == here, 1.0, 0.0)
        earlier = jnp.dot(onehot.astype(bf16), before, preferred_element_type=f32) + carry
        carry = carry + jnp.sum(onehot, axis=1, keepdims=True)
        rank = jnp.sum(onehot * earlier, axis=0, keepdims=True).astype(i32)
        slot_ref[:, start:start + BLOCK] = here * most + rank

    fetches[1].wait()
    key = key_ref[...]
    digit = lax.broadcasted_iota(i32, (SUB, rows), 0)
    digits = jnp.where(digit == 0, key // 16384, jnp.where(digit == 1, (key // 128) % 128, jnp.where(digit == 2, key % 128, jnp.where(digit == 3, 1, 0))))
    digits = digits.astype(f32).astype(bf16)

    place = lax.broadcasted_iota(i32, (SUB, SUB), 1)
    combine = jnp.where(place == 0, 16384.0, jnp.where(place == 1, 128.0, jnp.where(place == 2, 1.0, jnp.where(place == 3, -4194304.0, 0.0)))).astype(bf16)
    part = lax.broadcasted_iota(i32, (SUB, most), 0)

    def split3(whole):
        high = whole.astype(bf16).astype(f32)
        middle = (whole - high).astype(bf16).astype(f32)
        return high, middle, (whole - high) - middle

    def parts_of(row):
        high, middle, low = split3(jnp.broadcast_to(row, (SUB, most)))
        return jnp.where(part == 0, high, jnp.where(part == 1, middle, jnp.where(part == 2, low, 0.0)))

    same = lax.broadcasted_iota(i32, (most, most), 0) == lax.broadcasted_iota(i32, (most, most), 1)
    identity = jnp.where(same, 1.0, 0.0).astype(bf16)

    def pack(cluster):
        place = slot_ref[...] - cluster * most
        pick = jnp.where(lax.broadcasted_iota(i32, (most, rows), 0) == place, 1.0, 0.0).astype(bf16)
        values = jnp.dot(pick, rows_ref[...], preferred_element_type=f32)
        scale = lax.rsqrt(jnp.sum(values * values, axis=1, keepdims=True) + epsilon)
        picked = lax.dot_general(digits, pick, NT, preferred_element_type=f32)
        return (values * scale).astype(bf16), jnp.dot(combine, picked.astype(bf16), preferred_element_type=f32)[:1]

    def row_copy(offset):
        return pltpu.make_async_remote_copy(send.at[offset], recv.at[offset], row_ssem.at[offset], row_rsem.at[offset], device_id=device(offset), device_id_type=MESH)

    def key_copy(offset):
        return pltpu.make_async_remote_copy(send_key.at[offset], recv_key.at[offset], key_ssem.at[offset], key_rsem.at[offset], device_id=device(offset), device_id_type=MESH)

    def back_copy(offset, cluster):
        return pltpu.make_async_remote_copy(back_send.at[offset], back.at[cluster], back_ssem.at[offset], back_rsem.at[offset], device_id=device(offset), device_id_type=MESH)

    def fill(step):
        offset = sent(step)
        packed, packed_key = pack(xor(me, offset, n))
        send[offset] = packed
        send_key[offset] = packed_key

    fetches[2].wait()
    fill(jnp.int32(0))

    @pl.when(inner == 1)
    def _():
        pl.semaphore_wait(barrier, 2)

    @pl.when(inner == 0)
    def _():
        pl.semaphore_wait(barrier, n - 1)
        pl.semaphore_signal(go, inc=1, device_id=device(quarter), device_id_type=MESH)

    @pl.loop(1, n)
    def _(step):
        @pl.when(inner * step == 3)
        def _():
            pl.semaphore_wait(go, 1)

        offset = sent(step - 1)
        key_copy(offset).start()
        row_copy(offset).start()
        fill(step)

    for start in range(0, rows, BLOCK):
        rank = slot_ref[:, start:start + BLOCK] - cluster_ref[:, start:start + BLOCK] * most
        by_rank[:, start:start + BLOCK] = jnp.where(lax.broadcasted_iota(i32, (most, BLOCK), 0) == rank, 1.0, 0.0).astype(bf16)

    def take(offset, row):
        lane_key[offset] = jnp.broadcast_to(row, (SUB, most))
        turned = lax.dot_general(identity, parts_of(row).astype(bf16), NT, preferred_element_type=f32).astype(bf16)
        sub_key[...] = jnp.dot(turned, jnp.ones((SUB, most), bf16), preferred_element_type=f32)

    def highest(values):
        return jnp.max(values.reshape(most // SUB, SUB, most), axis=0)

    def alone(offset):
        block = recv[offset]
        sims = lax.dot_general(block, block, NT, preferred_element_type=f32)
        best[offset] = highest(jnp.where(sub_key[...] < lane_key[offset][:1], sims, -1.0))

    recv[0] = send[0]
    take(0, send_key[0])
    alone(0)

    @pl.loop(1, n)
    def _(step):
        u = taken(step)
        key_copy(u).wait_recv()
        take(u, recv_key[u])
        row_copy(u).wait_recv()
        alone(u)
        gather[...] = jnp.full((most, most), -1.0, f32)

        def meet(i):
            other = taken(i)
            sims = lax.dot_general(recv[u], recv[other], NT, preferred_element_type=f32)
            earlier = sub_key[...] < lane_key[other][:1]
            best[other] = jnp.maximum(best[other], highest(jnp.where(earlier, sims, -1.0)))
            return jnp.where(earlier, -1.0, sims)

        @pl.loop(0, step // GROUP)
        def _(group):
            seen = meet(group * GROUP)
            for i in range(1, GROUP):
                seen = jnp.maximum(seen, meet(group * GROUP + i))
            gather[...] = jnp.maximum(gather[...], seen)

        @pl.loop(step // GROUP * GROUP, step)
        def _(i):
            gather[...] = jnp.maximum(gather[...], meet(i))

        best[u] = jnp.maximum(best[u], highest(gather[...].T))

    for offset in range(n - 1, 0, -1):
        back_send[offset] = jnp.max(best[offset], axis=0, keepdims=True)
        back_copy(offset, me).start()
    back[me] = jnp.max(best[0], axis=0, keepdims=True)

    @pl.loop(1, n)
    def _(offset):
        row_copy(offset).wait_send()
        key_copy(offset).wait_send()

    for offset in range(1, n):
        back_copy(offset, flip(me, offset, n)).wait_recv()

    parts = jnp.concatenate(split3(back[...].reshape(n, most)), axis=0).astype(bf16)
    for start in range(0, rows, BLOCK):
        here = cluster_ref[:, start:start + BLOCK]
        found = jnp.dot(parts, by_rank[:, start:start + BLOCK], preferred_element_type=f32)
        whole = found[:n] + found[n:2 * n] + found[2 * n:]
        whole = jnp.where(lax.broadcasted_iota(i32, (n, BLOCK), 0) == here, whole, 0.0)
        out_ref[:, start:start + BLOCK] = jnp.sum(whole, axis=0, keepdims=True)

    for offset in range(1, n):
        back_copy(offset, me).wait_send()


def per_device(embeddings, assignment, order_key):
    rows, width = embeddings.shape
    n_split = lax.axis_size("split")
    n = lax.axis_size("dp") * n_split
    most = 3 * rows // (2 * n)
    f32, bf16 = jnp.float32, jnp.bfloat16
    vmem = pl.BlockSpec(memory_space=pltpu.VMEM)
    dma = pltpu.SemaphoreType.DMA((n,))
    nearest = pl.pallas_call(
        functools.partial(kernel, n, n_split, most),
        out_shape=jax.ShapeDtypeStruct((1, rows), f32),
        in_specs=[pl.BlockSpec(memory_space=pl.ANY)] * 3,
        out_specs=vmem,
        scratch_shapes=[
            pltpu.VMEM((rows, width), bf16),
            pltpu.VMEM((1, rows), jnp.int32),
            pltpu.VMEM((1, rows), jnp.int32),
            pltpu.SemaphoreType.DMA((3,)),
            pltpu.VMEM((1, rows), jnp.int32),
            pltpu.VMEM((n, most, width), bf16),
            pltpu.VMEM((n, 1, most), f32),
            pltpu.VMEM((n, most, width), bf16),
            pltpu.VMEM((n, 1, most), f32),
            pltpu.VMEM((n, SUB, most), f32),
            pltpu.VMEM((most, most), f32),
            pltpu.VMEM((n, SUB, most), f32),
            pltpu.VMEM((most, most), f32),
            pltpu.VMEM((n, 1, most), f32),
            pltpu.VMEM((n, 1, most), f32),
            pltpu.VMEM((most, rows), bf16),
            dma, dma, dma, dma, dma, dma,
            pltpu.SemaphoreType.REGULAR,
        ],
        compiler_params=pltpu.CompilerParams(collective_id=0, has_side_effects=True, vmem_limit_bytes=56 * 1024 * 1024),
    )(embeddings, assignment.reshape(1, rows), order_key.reshape(1, rows))
    return nearest.reshape(rows)


def solution(mesh):
    placed = (
        P(("groups", "dp", "split"), None),
        P(("groups", "dp", "split"), None),
        P(("groups", "dp", "split")),
    )
    return jax.shard_map(
        per_device,
        mesh=mesh,
        in_specs=placed,
        out_specs=P(("groups", "dp", "split")),
        check_vma=False,
    )
```

```python
import functools

import jax
import jax.numpy as jnp
from jax import lax
from jax.experimental import pallas as pl
from jax.experimental.pallas import tpu as pltpu
from jax.sharding import PartitionSpec as P

epsilon = 1e-06
MESH = pl.DeviceIdType.MESH
NT = (((1,), (1,)), ((), ()))
BLOCK = 256
SUB = 8
GROUP = 5


def xor(a, b, n):
    total, bit = 0, 1
    while bit < n:
        p, q = (a // bit) % 2, (b // bit) % 2
        total = total + (p + q - 2 * p * q) * bit
        bit *= 2
    return total


def flip(a, b, n):
    total, bit = 0, 1
    while bit < n:
        p = (a // bit) % 2
        total = total + (1 - p if b & bit else p) * bit
        bit *= 2
    return total


def entry(values, i):
    n, total = len(values), values[0] + i
    for k in range(1, n):
        jump = values[k] - values[k - 1] - 1
        if jump:
            total = total + jump * lax.div(i + (n - k), n)
    return total


def orders(n):
    q = n // 4
    same, near, far2, far3 = (list(range(max(1, i * q), i * q + q)) for i in range(4))
    send_outer = far2 + same + near + far3
    send_inner = far3[:2] + far2 + same + near + far3[2:]
    take_outer = [0] + same + near + far2[:q // 2] + far3 + far2[q // 2:]
    take_inner = [0] + same[:1] + far2[:-1] + same[1:-1] + far2[-1:] + far3[:1] + near[:1] + same[-1:] + far3[1:2] + near[1:] + far3[2:]
    return send_outer + [0], send_inner + [0], take_outer, take_inner


def kernel(n, n_split, most, rows_hbm, cluster_hbm, key_hbm, out_ref,
           rows_ref, cluster_ref, key_ref, fetch_sem, slot_ref, send, send_key, recv, recv_key, lane_key, sub_key, best, gather, back_send, back, by_rank,
           row_ssem, row_rsem, key_ssem, key_rsem, back_ssem, back_rsem, go):
    f32, bf16, i32 = jnp.float32, jnp.bfloat16, jnp.int32
    rows = rows_ref.shape[0]
    quarter = n // 4
    me = lax.axis_index("dp") * n_split + lax.axis_index("split")
    inner = (me // quarter // 2 + me // quarter) % 2
    barrier = pltpu.get_barrier_semaphore()

    def place_of(partner):
        return {"dp": partner // n_split, "split": partner % n_split}

    def device(offset):
        return place_of(flip(me, offset, n) if isinstance(offset, int) else xor(me, offset, n))

    def greet(offset):
        pl.semaphore_signal(barrier, inc=1, device_id=device(offset), device_id_type=MESH)

    fetches = [
        pltpu.make_async_copy(cluster_hbm, cluster_ref, fetch_sem.at[0]),
        pltpu.make_async_copy(key_hbm, key_ref, fetch_sem.at[1]),
        pltpu.make_async_copy(rows_hbm, rows_ref, fetch_sem.at[2]),
    ]
    for fetch in fetches:
        fetch.start()

    @pl.when(inner == 1)
    def _():
        for offset in [3 * quarter, 3 * quarter + 1] + list(range(3 * quarter - 1, quarter - 1, -1)):
            greet(offset)

    @pl.when(inner == 0)
    def _():
        for offset in list(range(n - 1, 3 * quarter - 1, -1)) + list(range(1, quarter)):
            greet(offset)

    send_outer, send_inner, take_outer, take_inner = orders(n)

    def either(outer_values, inner_values, i):
        first, second = entry(outer_values, i), entry(inner_values, i)
        return first + (second - first) * inner

    def sent(i):
        return either(send_outer, send_inner, i)

    def taken(i):
        return either(take_outer, take_inner, i)

    fetches[0].wait()
    before = (lax.broadcasted_iota(i32, (BLOCK, BLOCK), 0) < lax.broadcasted_iota(i32, (BLOCK, BLOCK), 1))
    before = jnp.where(before, 1.0, 0.0).astype(bf16)
    carry = jnp.zeros((n, 1), f32)
    for start in range(0, rows, BLOCK):
        here = cluster_ref[:, start:start + BLOCK]
        onehot = jnp.where(lax.broadcasted_iota(i32, (n, BLOCK), 0) == here, 1.0, 0.0)
        earlier = jnp.dot(onehot.astype(bf16), before, preferred_element_type=f32) + carry
        carry = carry + jnp.sum(onehot, axis=1, keepdims=True)
        rank = jnp.sum(onehot * earlier, axis=0, keepdims=True).astype(i32)
        slot_ref[:, start:start + BLOCK] = here * most + rank

    fetches[1].wait()
    key = key_ref[...]
    digit = lax.broadcasted_iota(i32, (SUB, rows), 0)
    digits = jnp.where(digit == 0, key // 16384, jnp.where(digit == 1, (key // 128) % 128, jnp.where(digit == 2, key % 128, jnp.where(digit == 3, 1, 0))))
    digits = digits.astype(f32).astype(bf16)

    place = lax.broadcasted_iota(i32, (SUB, SUB), 1)
    combine = jnp.where(place == 0, 16384.0, jnp.where(place == 1, 128.0, jnp.where(place == 2, 1.0, jnp.where(place == 3, -4194304.0, 0.0)))).astype(bf16)
    part = lax.broadcasted_iota(i32, (SUB, most), 0)

    def split3(whole):
        high = whole.astype(bf16).astype(f32)
        middle = (whole - high).astype(bf16).astype(f32)
        return high, middle, (whole - high) - middle

    def parts_of(row):
        high, middle, low = split3(jnp.broadcast_to(row, (SUB, most)))
        return jnp.where(part == 0, high, jnp.where(part == 1, middle, jnp.where(part == 2, low, 0.0)))

    same = lax.broadcasted_iota(i32, (most, most), 0) == lax.broadcasted_iota(i32, (most, most), 1)
    identity = jnp.where(same, 1.0, 0.0).astype(bf16)

    def pack(cluster):
        place = slot_ref[...] - cluster * most
        pick = jnp.where(lax.broadcasted_iota(i32, (most, rows), 0) == place, 1.0, 0.0).astype(bf16)
        values = jnp.dot(pick, rows_ref[...], preferred_element_type=f32)
        scale = lax.rsqrt(jnp.sum(values * values, axis=1, keepdims=True) + epsilon)
        picked = lax.dot_general(digits, pick, NT, preferred_element_type=f32)
        return (values * scale).astype(bf16), jnp.dot(combine, picked.astype(bf16), preferred_element_type=f32)[:1]

    def row_copy(offset):
        return pltpu.make_async_remote_copy(send.at[offset], recv.at[offset], row_ssem.at[offset], row_rsem.at[offset], device_id=device(offset), device_id_type=MESH)

    def key_copy(offset):
        return pltpu.make_async_remote_copy(send_key.at[offset], recv_key.at[offset], key_ssem.at[offset], key_rsem.at[offset], device_id=device(offset), device_id_type=MESH)

    def back_copy(offset, cluster):
        return pltpu.make_async_remote_copy(back_send.at[offset], back.at[cluster], back_ssem.at[offset], back_rsem.at[offset], device_id=device(offset), device_id_type=MESH)

    def fill(step):
        offset = sent(step)
        packed, packed_key = pack(xor(me, offset, n))
        send[offset] = packed
        send_key[offset] = packed_key

    fetches[2].wait()
    fill(jnp.int32(0))

    @pl.when(inner == 1)
    def _():
        pl.semaphore_wait(barrier, 2)

    @pl.when(inner == 0)
    def _():
        pl.semaphore_wait(barrier, n - 1)
        pl.semaphore_signal(go, inc=1, device_id=device(quarter), device_id_type=MESH)

    @pl.loop(1, n)
    def _(step):
        @pl.when(inner * step == 3)
        def _():
            pl.semaphore_wait(go, 1)

        offset = sent(step - 1)
        key_copy(offset).start()
        row_copy(offset).start()
        fill(step)

    for start in range(0, rows, BLOCK):
        rank = slot_ref[:, start:start + BLOCK] - cluster_ref[:, start:start + BLOCK] * most
        by_rank[:, start:start + BLOCK] = jnp.where(lax.broadcasted_iota(i32, (most, BLOCK), 0) == rank, 1.0, 0.0).astype(bf16)

    def take(offset, row):
        lane_key[offset] = jnp.broadcast_to(row, (SUB, most))
        turned = lax.dot_general(identity, parts_of(row).astype(bf16), NT, preferred_element_type=f32).astype(bf16)
        sub_key[...] = jnp.dot(turned, jnp.ones((SUB, most), bf16), preferred_element_type=f32)

    def highest(values):
        return jnp.max(values.reshape(most // SUB, SUB, most), axis=0)

    def alone(offset):
        block = recv[offset]
        sims = lax.dot_general(block, block, NT, preferred_element_type=f32)
        best[offset] = highest(jnp.where(sub_key[...] < lane_key[offset][:1], sims, -1.0))

    recv[0] = send[0]
    take(0, send_key[0])
    alone(0)

    @pl.loop(1, n)
    def _(step):
        u = taken(step)
        key_copy(u).wait_recv()
        take(u, recv_key[u])
        row_copy(u).wait_recv()
        alone(u)
        gather[...] = jnp.full((most, most), -1.0, f32)

        def meet(i):
            other = taken(i)
            sims = lax.dot_general(recv[u], recv[other], NT, preferred_element_type=f32)
            earlier = sub_key[...] < lane_key[other][:1]
            best[other] = jnp.maximum(best[other], highest(jnp.where(earlier, sims, -1.0)))
            return jnp.where(earlier, -1.0, sims)

        @pl.loop(0, step // GROUP)
        def _(group):
            seen = meet(group * GROUP)
            for i in range(1, GROUP):
                seen = jnp.maximum(seen, meet(group * GROUP + i))
            gather[...] = jnp.maximum(gather[...], seen)

        @pl.loop(step // GROUP * GROUP, step)
        def _(i):
            gather[...] = jnp.maximum(gather[...], meet(i))

        best[u] = jnp.maximum(best[u], highest(gather[...].T))

    back_send[...] = jnp.max(best[...], axis=1, keepdims=True)
    back[me] = jnp.max(best[0], axis=0, keepdims=True)
    for offset in range(n - 1, 0, -1):
        back_copy(offset, me).start()

    @pl.loop(1, n)
    def _(offset):
        row_copy(offset).wait_send()
        key_copy(offset).wait_send()

    for offset in range(1, n):
        back_copy(offset, flip(me, offset, n)).wait_recv()

    parts = jnp.concatenate(split3(back[...].reshape(n, most)), axis=0).astype(bf16)
    for start in range(0, rows, BLOCK):
        here = cluster_ref[:, start:start + BLOCK]
        found = jnp.dot(parts, by_rank[:, start:start + BLOCK], preferred_element_type=f32)
        whole = found[:n] + found[n:2 * n] + found[2 * n:]
        whole = jnp.where(lax.broadcasted_iota(i32, (n, BLOCK), 0) == here, whole, 0.0)
        out_ref[:, start:start + BLOCK] = jnp.sum(whole, axis=0, keepdims=True)

    for offset in range(1, n):
        back_copy(offset, me).wait_send()


def per_device(embeddings, assignment, order_key):
    rows, width = embeddings.shape
    n_split = lax.axis_size("split")
    n = lax.axis_size("dp") * n_split
    most = 3 * rows // (2 * n)
    f32, bf16 = jnp.float32, jnp.bfloat16
    vmem = pl.BlockSpec(memory_space=pltpu.VMEM)
    dma = pltpu.SemaphoreType.DMA((n,))
    nearest = pl.pallas_call(
        functools.partial(kernel, n, n_split, most),
        out_shape=pltpu.VMEM((1, rows), f32),
        in_specs=[pl.BlockSpec(memory_space=pl.ANY)] * 3,
        out_specs=vmem,
        scratch_shapes=[
            pltpu.VMEM((rows, width), bf16),
            pltpu.VMEM((1, rows), jnp.int32),
            pltpu.VMEM((1, rows), jnp.int32),
            pltpu.SemaphoreType.DMA((3,)),
            pltpu.VMEM((1, rows), jnp.int32),
            pltpu.VMEM((n, most, width), bf16),
            pltpu.VMEM((n, 1, most), f32),
            pltpu.VMEM((n, most, width), bf16),
            pltpu.VMEM((n, 1, most), f32),
            pltpu.VMEM((n, SUB, most), f32),
            pltpu.VMEM((most, most), f32),
            pltpu.VMEM((n, SUB, most), f32),
            pltpu.VMEM((most, most), f32),
            pltpu.VMEM((n, 1, most), f32),
            pltpu.VMEM((n, 1, most), f32),
            pltpu.VMEM((most, rows), bf16),
            dma, dma, dma, dma, dma, dma,
            pltpu.SemaphoreType.REGULAR,
        ],
        compiler_params=pltpu.CompilerParams(collective_id=0, has_side_effects=True, vmem_limit_bytes=56 * 1024 * 1024),
    )(embeddings, assignment.reshape(1, rows), order_key.reshape(1, rows))
    return nearest.reshape(rows)


def solution(mesh):
    placed = (
        P(("groups", "dp", "split"), None),
        P(("groups", "dp", "split"), None),
        P(("groups", "dp", "split")),
    )
    return jax.shard_map(
        per_device,
        mesh=mesh,
        in_specs=placed,
        out_specs=P(("groups", "dp", "split")),
        check_vma=False,
    )
```

```python
import functools

import jax
import jax.numpy as jnp
from jax import lax
from jax.experimental import pallas as pl
from jax.experimental.pallas import tpu as pltpu
from jax.sharding import PartitionSpec as P

epsilon = 1e-06
MESH = pl.DeviceIdType.MESH
NT = (((1,), (1,)), ((), ()))
BLOCK = 256
SUB = 8
GROUP = 5
PARTS = 2


def xor(a, b, n):
    total, bit = 0, 1
    while bit < n:
        p, q = (a // bit) % 2, (b // bit) % 2
        total = total + (p + q - 2 * p * q) * bit
        bit *= 2
    return total


def flip(a, b, n):
    total, bit = 0, 1
    while bit < n:
        p = (a // bit) % 2
        total = total + (1 - p if b & bit else p) * bit
        bit *= 2
    return total


def entry(values, i):
    n, total = len(values), values[0] + i
    for k in range(1, n):
        jump = values[k] - values[k - 1] - 1
        if jump:
            total = total + jump * lax.div(i + (n - k), n)
    return total


def orders(n):
    q = n // 4
    same, near, far2, far3 = (list(range(max(1, i * q), i * q + q)) for i in range(4))
    send_outer = far2 + same + near + far3
    send_inner = far3[:2] + far2 + same + near + far3[2:]
    take_outer = [0] + same + near + far2[:q // 2] + far3 + far2[q // 2:]
    take_inner = [0] + same[:1] + far2 + same[1:] + far3[:2] + near + far3[2:]
    return send_outer + [0], send_inner + [0], take_outer, take_inner


def kernel(n, n_split, most, rows_hbm, cluster_hbm, key_hbm, out_ref,
           rows_ref, cluster_ref, key_ref, fetch_sem, slot_ref, send, send_key, recv, recv_key, lane_key, sub_key, best, gather, back_send, back, by_rank,
           row_ssem, row_rsem, key_ssem, key_rsem, back_ssem, back_rsem, go):
    f32, bf16, i32 = jnp.float32, jnp.bfloat16, jnp.int32
    rows = rows_ref.shape[0]
    quarter = n // 4
    me = lax.axis_index("dp") * n_split + lax.axis_index("split")
    inner = (me // quarter // 2 + me // quarter) % 2
    barrier = pltpu.get_barrier_semaphore()

    def place_of(partner):
        return {"dp": partner // n_split, "split": partner % n_split}

    def device(offset):
        return place_of(flip(me, offset, n) if isinstance(offset, int) else xor(me, offset, n))

    def greet(offset):
        pl.semaphore_signal(barrier, inc=1, device_id=device(offset), device_id_type=MESH)

    part_rows = rows // PARTS
    fetches = [
        pltpu.make_async_copy(cluster_hbm, cluster_ref, fetch_sem.at[0]),
        pltpu.make_async_copy(key_hbm, key_ref, fetch_sem.at[1]),
    ] + [
        pltpu.make_async_copy(rows_hbm.at[pl.ds(i * part_rows, part_rows)], rows_ref.at[pl.ds(i * part_rows, part_rows)], fetch_sem.at[2 + i])
        for i in range(PARTS)
    ]
    for fetch in fetches:
        fetch.start()

    @pl.when(inner == 1)
    def _():
        for offset in [3 * quarter, 3 * quarter + 1] + list(range(3 * quarter - 1, quarter - 1, -1)):
            greet(offset)

    @pl.when(inner == 0)
    def _():
        for offset in list(range(n - 1, 3 * quarter - 1, -1)) + list(range(1, quarter)):
            greet(offset)

    send_outer, send_inner, take_outer, take_inner = orders(n)

    def either(outer_values, inner_values, i):
        first, second = entry(outer_values, i), entry(inner_values, i)
        return first + (second - first) * inner

    def sent(i):
        return either(send_outer, send_inner, i)

    def taken(i):
        return either(take_outer, take_inner, i)

    fetches[0].wait()
    before = (lax.broadcasted_iota(i32, (BLOCK, BLOCK), 0) < lax.broadcasted_iota(i32, (BLOCK, BLOCK), 1))
    before = jnp.where(before, 1.0, 0.0).astype(bf16)
    carry = jnp.zeros((n, 1), f32)
    for start in range(0, rows, BLOCK):
        here = cluster_ref[:, start:start + BLOCK]
        onehot = jnp.where(lax.broadcasted_iota(i32, (n, BLOCK), 0) == here, 1.0, 0.0)
        earlier = jnp.dot(onehot.astype(bf16), before, preferred_element_type=f32) + carry
        carry = carry + jnp.sum(onehot, axis=1, keepdims=True)
        rank = jnp.sum(onehot * earlier, axis=0, keepdims=True).astype(i32)
        slot_ref[:, start:start + BLOCK] = here * most + rank

    fetches[1].wait()
    key = key_ref[...]
    digit = lax.broadcasted_iota(i32, (SUB, rows), 0)
    digits = jnp.where(digit == 0, key // 16384, jnp.where(digit == 1, (key // 128) % 128, jnp.where(digit == 2, key % 128, jnp.where(digit == 3, 1, 0))))
    digits = digits.astype(f32).astype(bf16)

    place = lax.broadcasted_iota(i32, (SUB, SUB), 1)
    combine = jnp.where(place == 0, 16384.0, jnp.where(place == 1, 128.0, jnp.where(place == 2, 1.0, jnp.where(place == 3, -4194304.0, 0.0)))).astype(bf16)
    part = lax.broadcasted_iota(i32, (SUB, most), 0)

    def split3(whole):
        high = whole.astype(bf16).astype(f32)
        middle = (whole - high).astype(bf16).astype(f32)
        return high, middle, (whole - high) - middle

    def parts_of(row):
        high, middle, low = split3(jnp.broadcast_to(row, (SUB, most)))
        return jnp.where(part == 0, high, jnp.where(part == 1, middle, jnp.where(part == 2, low, 0.0)))

    same = lax.broadcasted_iota(i32, (most, most), 0) == lax.broadcasted_iota(i32, (most, most), 1)
    identity = jnp.where(same, 1.0, 0.0).astype(bf16)

    def pack(cluster, waits=()):
        place = slot_ref[...] - cluster * most
        pick = jnp.where(lax.broadcasted_iota(i32, (most, rows), 0) == place, 1.0, 0.0).astype(bf16)
        if waits:
            values = jnp.zeros((most, rows_ref.shape[1]), f32)
            for i, wait in enumerate(waits):
                wait()
                part = slice(i * part_rows, (i + 1) * part_rows)
                values = values + jnp.dot(pick[:, part], rows_ref[part], preferred_element_type=f32)
        else:
            values = jnp.dot(pick, rows_ref[...], preferred_element_type=f32)
        scale = lax.rsqrt(jnp.sum(values * values, axis=1, keepdims=True) + epsilon)
        picked = lax.dot_general(digits, pick, NT, preferred_element_type=f32)
        return (values * scale).astype(bf16), jnp.dot(combine, picked.astype(bf16), preferred_element_type=f32)[:1]

    def row_copy(offset):
        return pltpu.make_async_remote_copy(send.at[offset], recv.at[offset], row_ssem.at[offset], row_rsem.at[offset], device_id=device(offset), device_id_type=MESH)

    def key_copy(offset):
        return pltpu.make_async_remote_copy(send_key.at[offset], recv_key.at[offset], key_ssem.at[offset], key_rsem.at[offset], device_id=device(offset), device_id_type=MESH)

    def back_copy(offset, cluster):
        return pltpu.make_async_remote_copy(back_send.at[offset], back.at[cluster], back_ssem.at[offset], back_rsem.at[offset], device_id=device(offset), device_id_type=MESH)

    def fill(step, waits=()):
        offset = sent(step)
        packed, packed_key = pack(xor(me, offset, n), waits)
        send[offset] = packed
        send_key[offset] = packed_key

    fill(jnp.int32(0), [fetch.wait for fetch in fetches[2:]])

    @pl.when(inner == 1)
    def _():
        pl.semaphore_wait(barrier, 2)

    @pl.when(inner == 0)
    def _():
        pl.semaphore_wait(barrier, n - 1)
        pl.semaphore_signal(go, inc=1, device_id=device(quarter), device_id_type=MESH)

    @pl.loop(1, n)
    def _(step):
        @pl.when(inner * step == 3)
        def _():
            pl.semaphore_wait(go, 1)

        offset = sent(step - 1)
        key_copy(offset).start()
        row_copy(offset).start()
        fill(step)

    for start in range(0, rows, BLOCK):
        rank = slot_ref[:, start:start + BLOCK] - cluster_ref[:, start:start + BLOCK] * most
        by_rank[:, start:start + BLOCK] = jnp.where(lax.broadcasted_iota(i32, (most, BLOCK), 0) == rank, 1.0, 0.0).astype(bf16)

    def take(offset, row):
        lane_key[offset] = jnp.broadcast_to(row, (SUB, most))
        turned = lax.dot_general(identity, parts_of(row).astype(bf16), NT, preferred_element_type=f32).astype(bf16)
        sub_key[...] = jnp.dot(turned, jnp.ones((SUB, most), bf16), preferred_element_type=f32)

    def highest(values):
        return jnp.max(values.reshape(most // SUB, SUB, most), axis=0)

    def alone(offset):
        block = recv[offset]
        sims = lax.dot_general(block, block, NT, preferred_element_type=f32)
        best[offset] = highest(jnp.where(sub_key[...] < lane_key[offset][:1], sims, -1.0))

    recv[0] = send[0]
    take(0, send_key[0])
    alone(0)

    @pl.loop(1, n)
    def _(step):
        u = taken(step)
        key_copy(u).wait_recv()
        take(u, recv_key[u])
        row_copy(u).wait_recv()
        alone(u)
        gather[...] = jnp.full((most, most), -1.0, f32)

        def meet(i):
            other = taken(i)
            sims = lax.dot_general(recv[u], recv[other], NT, preferred_element_type=f32)
            earlier = sub_key[...] < lane_key[other][:1]
            best[other] = jnp.maximum(best[other], highest(jnp.where(earlier, sims, -1.0)))
            return jnp.where(earlier, -1.0, sims)

        @pl.loop(0, step // GROUP)
        def _(group):
            seen = meet(group * GROUP)
            for i in range(1, GROUP):
                seen = jnp.maximum(seen, meet(group * GROUP + i))
            gather[...] = jnp.maximum(gather[...], seen)

        @pl.loop(step // GROUP * GROUP, step)
        def _(i):
            gather[...] = jnp.maximum(gather[...], meet(i))

        best[u] = jnp.maximum(best[u], highest(gather[...].T))

    back_send[...] = jnp.max(best[...], axis=1, keepdims=True)
    back[me] = jnp.max(best[0], axis=0, keepdims=True)
    for offset in range(n - 1, 0, -1):
        back_copy(offset, me).start()

    @pl.loop(1, n)
    def _(offset):
        row_copy(offset).wait_send()
        key_copy(offset).wait_send()

    for offset in range(1, n):
        back_copy(offset, flip(me, offset, n)).wait_recv()

    parts = jnp.concatenate(split3(back[...].reshape(n, most)), axis=0).astype(bf16)
    for start in range(0, rows, BLOCK):
        here = cluster_ref[:, start:start + BLOCK]
        found = jnp.dot(parts, by_rank[:, start:start + BLOCK], preferred_element_type=f32)
        whole = found[:n] + found[n:2 * n] + found[2 * n:]
        whole = jnp.where(lax.broadcasted_iota(i32, (n, BLOCK), 0) == here, whole, 0.0)
        out_ref[:, start:start + BLOCK] = jnp.sum(whole, axis=0, keepdims=True)

    for offset in range(1, n):
        back_copy(offset, me).wait_send()


def per_device(embeddings, assignment, order_key):
    rows, width = embeddings.shape
    n_split = lax.axis_size("split")
    n = lax.axis_size("dp") * n_split
    most = 3 * rows // (2 * n)
    f32, bf16 = jnp.float32, jnp.bfloat16
    vmem = pl.BlockSpec(memory_space=pltpu.VMEM)
    dma = pltpu.SemaphoreType.DMA((n,))
    nearest = pl.pallas_call(
        functools.partial(kernel, n, n_split, most),
        out_shape=pltpu.VMEM((1, rows), f32),
        in_specs=[pl.BlockSpec(memory_space=pl.ANY)] * 3,
        out_specs=vmem,
        scratch_shapes=[
            pltpu.VMEM((rows, width), bf16),
            pltpu.VMEM((1, rows), jnp.int32),
            pltpu.VMEM((1, rows), jnp.int32),
            pltpu.SemaphoreType.DMA((2 + PARTS,)),
            pltpu.VMEM((1, rows), jnp.int32),
            pltpu.VMEM((n, most, width), bf16),
            pltpu.VMEM((n, 1, most), f32),
            pltpu.VMEM((n, most, width), bf16),
            pltpu.VMEM((n, 1, most), f32),
            pltpu.VMEM((n, SUB, most), f32),
            pltpu.VMEM((most, most), f32),
            pltpu.VMEM((n, SUB, most), f32),
            pltpu.VMEM((most, most), f32),
            pltpu.VMEM((n, 1, most), f32),
            pltpu.VMEM((n, 1, most), f32),
            pltpu.VMEM((most, rows), bf16),
            dma, dma, dma, dma, dma, dma,
            pltpu.SemaphoreType.REGULAR,
        ],
        compiler_params=pltpu.CompilerParams(collective_id=0, has_side_effects=True, vmem_limit_bytes=56 * 1024 * 1024),
    )(embeddings, assignment.reshape(1, rows), order_key.reshape(1, rows))
    return nearest.reshape(rows)


def solution(mesh):
    placed = (
        P(("groups", "dp", "split"), None),
        P(("groups", "dp", "split"), None),
        P(("groups", "dp", "split")),
    )
    return jax.shard_map(
        per_device,
        mesh=mesh,
        in_specs=placed,
        out_specs=P(("groups", "dp", "split")),
        check_vma=False,
    )
```

```python
import functools

import jax
import jax.numpy as jnp
from jax import lax
from jax.experimental import pallas as pl
from jax.experimental.pallas import tpu as pltpu
from jax.sharding import PartitionSpec as P

epsilon = 1e-06
MESH = pl.DeviceIdType.MESH
NT = (((1,), (1,)), ((), ()))
BLOCK = 256
SUB = 8
GROUP = 5
PARTS = 2


def xor(a, b, n):
    total, bit = 0, 1
    while bit < n:
        p, q = (a // bit) % 2, (b // bit) % 2
        total = total + (p + q - 2 * p * q) * bit
        bit *= 2
    return total


def flip(a, b, n):
    total, bit = 0, 1
    while bit < n:
        p = (a // bit) % 2
        total = total + (1 - p if b & bit else p) * bit
        bit *= 2
    return total


def entry(values, i):
    n, total = len(values), values[0] + i
    for k in range(1, n):
        jump = values[k] - values[k - 1] - 1
        if jump:
            total = total + jump * lax.div(i + (n - k), n)
    return total


def orders(n):
    q = n // 4
    same, near, far2, far3 = (list(range(max(1, i * q), i * q + q)) for i in range(4))
    send_outer = far2 + same + near + far3
    send_inner = far3[:2] + far2 + same + near + far3[2:]
    take_outer = [0] + same + near + far2[:q // 2] + far3 + far2[q // 2:]
    take_inner = [0] + same[:1] + far2 + same[1:] + far3[:2] + near + far3[2:]
    return send_outer + [0], send_inner + [0], take_outer, take_inner


def kernel(n, n_split, most, rows_hbm, cluster_hbm, key_hbm, out_ref,
           rows_ref, cluster_ref, key_ref, fetch_sem, slot_ref, send, send_key, recv, recv_key, lane_key, sub_key, best, gather, back_send, back, by_rank,
           row_ssem, row_rsem, key_ssem, key_rsem, back_ssem, back_rsem, go):
    f32, bf16, i32 = jnp.float32, jnp.bfloat16, jnp.int32
    rows = rows_ref.shape[0]
    quarter = n // 4
    me = lax.axis_index("dp") * n_split + lax.axis_index("split")
    inner = (me // quarter // 2 + me // quarter) % 2
    barrier = pltpu.get_barrier_semaphore()

    def place_of(partner):
        return {"dp": partner // n_split, "split": partner % n_split}

    def device(offset):
        return place_of(flip(me, offset, n) if isinstance(offset, int) else xor(me, offset, n))

    def greet(offset):
        pl.semaphore_signal(barrier, inc=1, device_id=device(offset), device_id_type=MESH)

    part_rows = rows // PARTS
    fetches = [
        pltpu.make_async_copy(cluster_hbm, cluster_ref, fetch_sem.at[0]),
        pltpu.make_async_copy(key_hbm, key_ref, fetch_sem.at[1]),
    ] + [
        pltpu.make_async_copy(rows_hbm.at[pl.ds(i * part_rows, part_rows)], rows_ref.at[pl.ds(i * part_rows, part_rows)], fetch_sem.at[2 + i])
        for i in range(PARTS)
    ]
    for fetch in fetches:
        fetch.start()

    @pl.when(inner == 1)
    def _():
        for offset in [3 * quarter, 3 * quarter + 1] + list(range(3 * quarter - 1, quarter - 1, -1)):
            greet(offset)

    @pl.when(inner == 0)
    def _():
        for offset in list(range(n - 1, 3 * quarter - 1, -1)) + list(range(1, quarter)):
            greet(offset)

    send_outer, send_inner, take_outer, take_inner = orders(n)

    def either(outer_values, inner_values, i):
        first, second = entry(outer_values, i), entry(inner_values, i)
        return first + (second - first) * inner

    def sent(i):
        return either(send_outer, send_inner, i)

    def taken(i):
        return either(take_outer, take_inner, i)

    fetches[0].wait()
    before = (lax.broadcasted_iota(i32, (BLOCK, BLOCK), 0) < lax.broadcasted_iota(i32, (BLOCK, BLOCK), 1))
    before = jnp.where(before, 1.0, 0.0).astype(bf16)
    carry = jnp.zeros((n, 1), f32)
    for start in range(0, rows, BLOCK):
        here = cluster_ref[:, start:start + BLOCK]
        onehot = jnp.where(lax.broadcasted_iota(i32, (n, BLOCK), 0) == here, 1.0, 0.0)
        earlier = jnp.dot(onehot.astype(bf16), before, preferred_element_type=f32) + carry
        carry = carry + jnp.sum(onehot, axis=1, keepdims=True)
        rank = jnp.sum(onehot * earlier, axis=0, keepdims=True).astype(i32)
        slot_ref[:, start:start + BLOCK] = here * most + rank

    fetches[1].wait()
    key = key_ref[...]
    digit = lax.broadcasted_iota(i32, (SUB, rows), 0)
    digits = jnp.where(digit == 0, key // 16384, jnp.where(digit == 1, (key // 128) % 128, jnp.where(digit == 2, key % 128, jnp.where(digit == 3, 1, 0))))
    digits = digits.astype(f32).astype(bf16)

    place = lax.broadcasted_iota(i32, (SUB, SUB), 1)
    combine = jnp.where(place == 0, 16384.0, jnp.where(place == 1, 128.0, jnp.where(place == 2, 1.0, jnp.where(place == 3, -4194304.0, 0.0)))).astype(bf16)
    part = lax.broadcasted_iota(i32, (SUB, most), 0)

    def split3(whole):
        high = whole.astype(bf16).astype(f32)
        middle = (whole - high).astype(bf16).astype(f32)
        return high, middle, (whole - high) - middle

    def parts_of(row):
        high, middle, low = split3(jnp.broadcast_to(row, (SUB, most)))
        return jnp.where(part == 0, high, jnp.where(part == 1, middle, jnp.where(part == 2, low, 0.0)))

    same = lax.broadcasted_iota(i32, (most, most), 0) == lax.broadcasted_iota(i32, (most, most), 1)
    identity = jnp.where(same, 1.0, 0.0).astype(bf16)

    def pack(cluster, waits=()):
        place = slot_ref[...] - cluster * most
        pick = jnp.where(lax.broadcasted_iota(i32, (most, rows), 0) == place, 1.0, 0.0).astype(bf16)
        if waits:
            values = jnp.zeros((most, rows_ref.shape[1]), f32)
            for i, wait in enumerate(waits):
                wait()
                part = slice(i * part_rows, (i + 1) * part_rows)
                values = values + jnp.dot(pick[:, part], rows_ref[part], preferred_element_type=f32)
        else:
            values = jnp.dot(pick, rows_ref[...], preferred_element_type=f32)
        scale = lax.rsqrt(jnp.sum(values * values, axis=1, keepdims=True) + epsilon)
        return (values * scale).astype(bf16), pick

    def keys_of(pick):
        picked = lax.dot_general(digits, pick, NT, preferred_element_type=f32)
        return jnp.dot(combine, picked.astype(bf16), preferred_element_type=f32)[:1]

    def row_copy(offset):
        return pltpu.make_async_remote_copy(send.at[offset], recv.at[offset], row_ssem.at[offset], row_rsem.at[offset], device_id=device(offset), device_id_type=MESH)

    def key_copy(offset):
        return pltpu.make_async_remote_copy(send_key.at[offset], recv_key.at[offset], key_ssem.at[offset], key_rsem.at[offset], device_id=device(offset), device_id_type=MESH)

    def back_copy(offset, cluster):
        return pltpu.make_async_remote_copy(back_send.at[offset], back.at[cluster], back_ssem.at[offset], back_rsem.at[offset], device_id=device(offset), device_id_type=MESH)

    def fill(step, waits=()):
        offset = sent(step)
        packed, pick = pack(xor(me, offset, n), waits)
        send[offset] = packed
        return pick

    first = sent(jnp.int32(0))
    pick = fill(jnp.int32(0), [fetch.wait for fetch in fetches[2:]])

    @pl.when(inner == 1)
    def _():
        pl.semaphore_wait(barrier, 2)

    @pl.when(inner == 0)
    def _():
        pl.semaphore_wait(barrier, n - 1)
        pl.semaphore_signal(go, inc=1, device_id=device(quarter), device_id_type=MESH)

    row_copy(first).start()
    send_key[first] = keys_of(pick)

    @pl.loop(1, n)
    def _(step):
        @pl.when(inner * step == 3)
        def _():
            pl.semaphore_wait(go, 1)

        offset = sent(step - 1)
        key_copy(offset).start()

        @pl.when(step > 1)
        def _():
            row_copy(offset).start()

        send_key[sent(step)] = keys_of(fill(step))

    for start in range(0, rows, BLOCK):
        rank = slot_ref[:, start:start + BLOCK] - cluster_ref[:, start:start + BLOCK] * most
        by_rank[:, start:start + BLOCK] = jnp.where(lax.broadcasted_iota(i32, (most, BLOCK), 0) == rank, 1.0, 0.0).astype(bf16)

    def take(offset, row):
        lane_key[offset] = jnp.broadcast_to(row, (SUB, most))
        turned = lax.dot_general(identity, parts_of(row).astype(bf16), NT, preferred_element_type=f32).astype(bf16)
        sub_key[...] = jnp.dot(turned, jnp.ones((SUB, most), bf16), preferred_element_type=f32)

    def highest(values):
        return jnp.max(values.reshape(most // SUB, SUB, most), axis=0)

    def alone(offset):
        block = recv[offset]
        sims = lax.dot_general(block, block, NT, preferred_element_type=f32)
        best[offset] = highest(jnp.where(sub_key[...] < lane_key[offset][:1], sims, -1.0))

    recv[0] = send[0]
    take(0, send_key[0])
    alone(0)

    @pl.loop(1, n)
    def _(step):
        u = taken(step)
        key_copy(u).wait_recv()
        take(u, recv_key[u])
        row_copy(u).wait_recv()
        alone(u)
        gather[...] = jnp.full((most, most), -1.0, f32)

        def meet(i):
            other = taken(i)
            sims = lax.dot_general(recv[u], recv[other], NT, preferred_element_type=f32)
            earlier = sub_key[...] < lane_key[other][:1]
            best[other] = jnp.maximum(best[other], highest(jnp.where(earlier, sims, -1.0)))
            return jnp.where(earlier, -1.0, sims)

        @pl.loop(0, step // GROUP)
        def _(group):
            seen = meet(group * GROUP)
            for i in range(1, GROUP):
                seen = jnp.maximum(seen, meet(group * GROUP + i))
            gather[...] = jnp.maximum(gather[...], seen)

        @pl.loop(step // GROUP * GROUP, step)
        def _(i):
            gather[...] = jnp.maximum(gather[...], meet(i))

        best[u] = jnp.maximum(best[u], highest(gather[...].T))

    back_send[...] = jnp.max(best[...], axis=1, keepdims=True)
    back[me] = jnp.max(best[0], axis=0, keepdims=True)
    for offset in range(n - 1, 0, -1):
        back_copy(offset, me).start()

    @pl.loop(1, n)
    def _(offset):
        row_copy(offset).wait_send()
        key_copy(offset).wait_send()

    for offset in range(1, n):
        back_copy(offset, flip(me, offset, n)).wait_recv()

    parts = jnp.concatenate(split3(back[...].reshape(n, most)), axis=0).astype(bf16)
    for start in range(0, rows, BLOCK):
        here = cluster_ref[:, start:start + BLOCK]
        found = jnp.dot(parts, by_rank[:, start:start + BLOCK], preferred_element_type=f32)
        whole = found[:n] + found[n:2 * n] + found[2 * n:]
        whole = jnp.where(lax.broadcasted_iota(i32, (n, BLOCK), 0) == here, whole, 0.0)
        out_ref[:, start:start + BLOCK] = jnp.sum(whole, axis=0, keepdims=True)

    for offset in range(1, n):
        back_copy(offset, me).wait_send()


def per_device(embeddings, assignment, order_key):
    rows, width = embeddings.shape
    n_split = lax.axis_size("split")
    n = lax.axis_size("dp") * n_split
    most = 3 * rows // (2 * n)
    f32, bf16 = jnp.float32, jnp.bfloat16
    vmem = pl.BlockSpec(memory_space=pltpu.VMEM)
    dma = pltpu.SemaphoreType.DMA((n,))
    nearest = pl.pallas_call(
        functools.partial(kernel, n, n_split, most),
        out_shape=pltpu.VMEM((1, rows), f32),
        in_specs=[pl.BlockSpec(memory_space=pl.ANY)] * 3,
        out_specs=vmem,
        scratch_shapes=[
            pltpu.VMEM((rows, width), bf16),
            pltpu.VMEM((1, rows), jnp.int32),
            pltpu.VMEM((1, rows), jnp.int32),
            pltpu.SemaphoreType.DMA((2 + PARTS,)),
            pltpu.VMEM((1, rows), jnp.int32),
            pltpu.VMEM((n, most, width), bf16),
            pltpu.VMEM((n, 1, most), f32),
            pltpu.VMEM((n, most, width), bf16),
            pltpu.VMEM((n, 1, most), f32),
            pltpu.VMEM((n, SUB, most), f32),
            pltpu.VMEM((most, most), f32),
            pltpu.VMEM((n, SUB, most), f32),
            pltpu.VMEM((most, most), f32),
            pltpu.VMEM((n, 1, most), f32),
            pltpu.VMEM((n, 1, most), f32),
            pltpu.VMEM((most, rows), bf16),
            dma, dma, dma, dma, dma, dma,
            pltpu.SemaphoreType.REGULAR,
        ],
        compiler_params=pltpu.CompilerParams(collective_id=0, has_side_effects=True, vmem_limit_bytes=56 * 1024 * 1024),
    )(embeddings, assignment.reshape(1, rows), order_key.reshape(1, rows))
    return nearest.reshape(rows)


def solution(mesh):
    placed = (
        P(("groups", "dp", "split"), None),
        P(("groups", "dp", "split"), None),
        P(("groups", "dp", "split")),
    )
    return jax.shard_map(
        per_device,
        mesh=mesh,
        in_specs=placed,
        out_specs=P(("groups", "dp", "split")),
        check_vma=False,
    )
```

```python
import functools

import jax
import jax.numpy as jnp
from jax import lax
from jax.experimental import pallas as pl
from jax.experimental.pallas import tpu as pltpu
from jax.sharding import PartitionSpec as P

epsilon = 1e-06
MESH = pl.DeviceIdType.MESH
NT = (((1,), (1,)), ((), ()))
BLOCK = 256
SUB = 8
GROUP = 5
PARTS = 2


def xor(a, b, n):
    total, bit = 0, 1
    while bit < n:
        p, q = (a // bit) % 2, (b // bit) % 2
        total = total + (p + q - 2 * p * q) * bit
        bit *= 2
    return total


def flip(a, b, n):
    total, bit = 0, 1
    while bit < n:
        p = (a // bit) % 2
        total = total + (1 - p if b & bit else p) * bit
        bit *= 2
    return total


def entry(values, i):
    n, total = len(values), values[0] + i
    for k in range(1, n):
        jump = values[k] - values[k - 1] - 1
        if jump:
            total = total + jump * lax.div(i + (n - k), n)
    return total


def orders(n):
    q = n // 4
    same, near, far2, far3 = (list(range(max(1, i * q), i * q + q)) for i in range(4))
    send_outer = far2 + same + near + far3
    send_inner = far3[:2] + far2 + same + near + far3[2:]
    take_outer = [0] + same + near + far2[:q // 2] + far3 + far2[q // 2:]
    take_inner = [0] + same[:1] + far2 + same[1:] + far3[:2] + near + far3[2:]
    return send_outer + [0], send_inner + [0], take_outer, take_inner


def kernel(n, n_split, most, rows_hbm, cluster_hbm, key_hbm, out_ref,
           rows_ref, cluster_ref, key_ref, fetch_sem, slot_ref, send, send_key, recv, recv_key, lane_key, sub_key, best, gather, back_send, back, by_rank,
           row_ssem, row_rsem, key_ssem, key_rsem, back_ssem, back_rsem, go):
    f32, bf16, i32 = jnp.float32, jnp.bfloat16, jnp.int32
    rows = rows_ref.shape[0]
    quarter = n // 4
    me = lax.axis_index("dp") * n_split + lax.axis_index("split")
    inner = (me // quarter // 2 + me // quarter) % 2
    barrier = pltpu.get_barrier_semaphore()

    def place_of(partner):
        return {"dp": partner // n_split, "split": partner % n_split}

    def device(offset):
        return place_of(flip(me, offset, n) if isinstance(offset, int) else xor(me, offset, n))

    def greet(offset):
        pl.semaphore_signal(barrier, inc=1, device_id=device(offset), device_id_type=MESH)

    part_rows = rows // PARTS
    fetches = [
        pltpu.make_async_copy(cluster_hbm, cluster_ref, fetch_sem.at[0]),
        pltpu.make_async_copy(key_hbm, key_ref, fetch_sem.at[1]),
    ] + [
        pltpu.make_async_copy(rows_hbm.at[pl.ds(i * part_rows, part_rows)], rows_ref.at[pl.ds(i * part_rows, part_rows)], fetch_sem.at[2 + i])
        for i in range(PARTS)
    ]
    for fetch in fetches:
        fetch.start()

    @pl.when(inner == 1)
    def _():
        for offset in [3 * quarter, 3 * quarter + 1] + list(range(3 * quarter - 1, quarter - 1, -1)):
            greet(offset)

    @pl.when(inner == 0)
    def _():
        for offset in list(range(n - 1, 3 * quarter - 1, -1)) + list(range(1, quarter)):
            greet(offset)

    send_outer, send_inner, take_outer, take_inner = orders(n)

    def either(outer_values, inner_values, i):
        first, second = entry(outer_values, i), entry(inner_values, i)
        return first + (second - first) * inner

    def sent(i):
        return either(send_outer, send_inner, i)

    def taken(i):
        return either(take_outer, take_inner, i)

    fetches[0].wait()
    before = (lax.broadcasted_iota(i32, (BLOCK, BLOCK), 0) < lax.broadcasted_iota(i32, (BLOCK, BLOCK), 1))
    before = jnp.where(before, 1.0, 0.0).astype(bf16)
    carry = jnp.zeros((n, 1), f32)
    for start in range(0, rows, BLOCK):
        here = cluster_ref[:, start:start + BLOCK]
        onehot = jnp.where(lax.broadcasted_iota(i32, (n, BLOCK), 0) == here, 1.0, 0.0)
        earlier = jnp.dot(onehot.astype(bf16), before, preferred_element_type=f32) + carry
        carry = carry + jnp.sum(onehot, axis=1, keepdims=True)
        rank = jnp.sum(onehot * earlier, axis=0, keepdims=True).astype(i32)
        slot_ref[:, start:start + BLOCK] = here * most + rank

    fetches[1].wait()
    key = key_ref[...]
    digit = lax.broadcasted_iota(i32, (SUB, rows), 0)
    digits = jnp.where(digit == 0, key // 16384, jnp.where(digit == 1, (key // 128) % 128, jnp.where(digit == 2, key % 128, jnp.where(digit == 3, 1, 0))))
    digits = digits.astype(f32).astype(bf16)

    place = lax.broadcasted_iota(i32, (SUB, SUB), 1)
    combine = jnp.where(place == 0, 16384.0, jnp.where(place == 1, 128.0, jnp.where(place == 2, 1.0, jnp.where(place == 3, -4194304.0, 0.0)))).astype(bf16)
    part = lax.broadcasted_iota(i32, (SUB, most), 0)

    def split3(whole):
        high = whole.astype(bf16).astype(f32)
        middle = (whole - high).astype(bf16).astype(f32)
        return high, middle, (whole - high) - middle

    def parts_of(row):
        high, middle, low = split3(jnp.broadcast_to(row, (SUB, most)))
        return jnp.where(part == 0, high, jnp.where(part == 1, middle, jnp.where(part == 2, low, 0.0)))

    same = lax.broadcasted_iota(i32, (most, most), 0) == lax.broadcasted_iota(i32, (most, most), 1)
    identity = jnp.where(same, 1.0, 0.0).astype(bf16)

    def pack(cluster, waits=()):
        place = slot_ref[...] - cluster * most
        pick = jnp.where(lax.broadcasted_iota(i32, (most, rows), 0) == place, 1.0, 0.0).astype(bf16)
        if waits:
            values = jnp.zeros((most, rows_ref.shape[1]), f32)
            for i, wait in enumerate(waits):
                wait()
                part = slice(i * part_rows, (i + 1) * part_rows)
                values = values + jnp.dot(pick[:, part], rows_ref[part], preferred_element_type=f32)
        else:
            values = jnp.dot(pick, rows_ref[...], preferred_element_type=f32)
        scale = lax.rsqrt(jnp.sum(values * values, axis=1, keepdims=True) + epsilon)
        picked = lax.dot_general(digits, pick, NT, preferred_element_type=f32)
        return (values * scale).astype(bf16), jnp.dot(combine, picked.astype(bf16), preferred_element_type=f32)[:1]

    def row_copy(offset):
        return pltpu.make_async_remote_copy(send.at[offset], recv.at[offset], row_ssem.at[offset], row_rsem.at[offset], device_id=device(offset), device_id_type=MESH)

    def key_copy(offset):
        return pltpu.make_async_remote_copy(send_key.at[offset], recv_key.at[offset], key_ssem.at[offset], key_rsem.at[offset], device_id=device(offset), device_id_type=MESH)

    def back_copy(offset, cluster):
        return pltpu.make_async_remote_copy(back_send.at[offset], back.at[cluster], back_ssem.at[offset], back_rsem.at[offset], device_id=device(offset), device_id_type=MESH)

    def fill(step, waits=()):
        offset = sent(step)
        packed, packed_key = pack(xor(me, offset, n), waits)
        send[offset] = packed
        send_key[offset] = packed_key

    fill(jnp.int32(0), [fetch.wait for fetch in fetches[2:]])

    @pl.when(inner == 1)
    def _():
        pl.semaphore_wait(barrier, 2)

    @pl.when(inner == 0)
    def _():
        pl.semaphore_wait(barrier, n - 1)
        pl.semaphore_signal(go, inc=1, device_id=device(quarter), device_id_type=MESH)

    def advance(step):
        offset = sent(step - 1)
        key_copy(offset).start()
        row_copy(offset).start()
        fill(step)

    pl.loop(1, 3)(advance)

    @pl.when(inner == 1)
    def _():
        pl.semaphore_wait(go, 1)

    pl.loop(3, n)(advance)

    for start in range(0, rows, BLOCK):
        rank = slot_ref[:, start:start + BLOCK] - cluster_ref[:, start:start + BLOCK] * most
        by_rank[:, start:start + BLOCK] = jnp.where(lax.broadcasted_iota(i32, (most, BLOCK), 0) == rank, 1.0, 0.0).astype(bf16)

    def take(offset, row):
        lane_key[offset] = jnp.broadcast_to(row, (SUB, most))
        turned = lax.dot_general(identity, parts_of(row).astype(bf16), NT, preferred_element_type=f32).astype(bf16)
        sub_key[...] = jnp.dot(turned, jnp.ones((SUB, most), bf16), preferred_element_type=f32)

    def highest(values):
        return jnp.max(values.reshape(most // SUB, SUB, most), axis=0)

    def alone(offset):
        block = recv[offset]
        sims = lax.dot_general(block, block, NT, preferred_element_type=f32)
        best[offset] = highest(jnp.where(sub_key[...] < lane_key[offset][:1], sims, -1.0))

    recv[0] = send[0]
    take(0, send_key[0])
    alone(0)

    @pl.loop(1, n)
    def _(step):
        u = taken(step)
        key_copy(u).wait_recv()
        take(u, recv_key[u])
        row_copy(u).wait_recv()
        alone(u)
        gather[...] = jnp.full((most, most), -1.0, f32)

        def meet(i):
            other = taken(i)
            sims = lax.dot_general(recv[u], recv[other], NT, preferred_element_type=f32)
            earlier = sub_key[...] < lane_key[other][:1]
            best[other] = jnp.maximum(best[other], highest(jnp.where(earlier, sims, -1.0)))
            return jnp.where(earlier, -1.0, sims)

        @pl.loop(0, step // GROUP)
        def _(group):
            seen = meet(group * GROUP)
            for i in range(1, GROUP):
                seen = jnp.maximum(seen, meet(group * GROUP + i))
            gather[...] = jnp.maximum(gather[...], seen)

        @pl.loop(step // GROUP * GROUP, step)
        def _(i):
            gather[...] = jnp.maximum(gather[...], meet(i))

        best[u] = jnp.maximum(best[u], highest(gather[...].T))

    back_send[...] = jnp.max(best[...], axis=1, keepdims=True)
    back[me] = jnp.max(best[0], axis=0, keepdims=True)
    for offset in range(n - 1, 0, -1):
        back_copy(offset, me).start()

    @pl.loop(1, n)
    def _(offset):
        row_copy(offset).wait_send()
        key_copy(offset).wait_send()

    for offset in range(1, n):
        back_copy(offset, flip(me, offset, n)).wait_recv()

    parts = jnp.concatenate(split3(back[...].reshape(n, most)), axis=0).astype(bf16)
    for start in range(0, rows, BLOCK):
        here = cluster_ref[:, start:start + BLOCK]
        found = jnp.dot(parts, by_rank[:, start:start + BLOCK], preferred_element_type=f32)
        whole = found[:n] + found[n:2 * n] + found[2 * n:]
        whole = jnp.where(lax.broadcasted_iota(i32, (n, BLOCK), 0) == here, whole, 0.0)
        out_ref[:, start:start + BLOCK] = jnp.sum(whole, axis=0, keepdims=True)

    for offset in range(1, n):
        back_copy(offset, me).wait_send()


def per_device(embeddings, assignment, order_key):
    rows, width = embeddings.shape
    n_split = lax.axis_size("split")
    n = lax.axis_size("dp") * n_split
    most = 3 * rows // (2 * n)
    f32, bf16 = jnp.float32, jnp.bfloat16
    vmem = pl.BlockSpec(memory_space=pltpu.VMEM)
    dma = pltpu.SemaphoreType.DMA((n,))
    nearest = pl.pallas_call(
        functools.partial(kernel, n, n_split, most),
        out_shape=pltpu.VMEM((1, rows), f32),
        in_specs=[pl.BlockSpec(memory_space=pl.ANY)] * 3,
        out_specs=vmem,
        scratch_shapes=[
            pltpu.VMEM((rows, width), bf16),
            pltpu.VMEM((1, rows), jnp.int32),
            pltpu.VMEM((1, rows), jnp.int32),
            pltpu.SemaphoreType.DMA((2 + PARTS,)),
            pltpu.VMEM((1, rows), jnp.int32),
            pltpu.VMEM((n, most, width), bf16),
            pltpu.VMEM((n, 1, most), f32),
            pltpu.VMEM((n, most, width), bf16),
            pltpu.VMEM((n, 1, most), f32),
            pltpu.VMEM((n, SUB, most), f32),
            pltpu.VMEM((most, most), f32),
            pltpu.VMEM((n, SUB, most), f32),
            pltpu.VMEM((most, most), f32),
            pltpu.VMEM((n, 1, most), f32),
            pltpu.VMEM((n, 1, most), f32),
            pltpu.VMEM((most, rows), bf16),
            dma, dma, dma, dma, dma, dma,
            pltpu.SemaphoreType.REGULAR,
        ],
        compiler_params=pltpu.CompilerParams(collective_id=0, has_side_effects=True, vmem_limit_bytes=56 * 1024 * 1024),
    )(embeddings, assignment.reshape(1, rows), order_key.reshape(1, rows))
    return nearest.reshape(rows)


def solution(mesh):
    placed = (
        P(("groups", "dp", "split"), None),
        P(("groups", "dp", "split"), None),
        P(("groups", "dp", "split")),
    )
    return jax.shard_map(
        per_device,
        mesh=mesh,
        in_specs=placed,
        out_specs=P(("groups", "dp", "split")),
        check_vma=False,
    )
```
